32 devices in a mesh: pop: 16 (over z, y, core), tp: 2 (over x).
Axes of the slice: x: 2, y: 2, z: 4, core: 2. Of those that a mesh axis runs over, the one named last changes fastest.
Arguments:
- tokens: bfloat16 [16, 512, 1792], P('pop', None, 'tp'), may hold values from -6 to 6
- weight: bfloat16 [16, 1792, 7168], P('pop', 'tp'), may hold values from -0.125 to 0.125
- momentum: bfloat16 [16, 1792, 7168], P('pop', 'tp'), may hold values from -6 to 6
- cotangent: bfloat16 [16, 512, 7168], P('pop', None, 'tp'), may hold values from -0.5 to 0.5
- assignment: int32 [4, 2], replicated, may hold values from 0 to 15, as said below
- lr_index: int32 [16], replicated, may hold values from 0 to 7
- rates: float32 [8], replicated, may hold values from 0.01 to 0.1
Outputs:
- activation: bfloat16 [16, 512, 7168], P('pop', None, 'tp')
- new_weight: bfloat16 [16, 1792, 7168], P('pop', 'tp')
The draws below stay inside these ranges and needn't reach their ends.
Inputs may be any that keep to these rules, and one draw needn't show every extreme that they name: `assignment`: column 0 names 4 distinct members; column 1 names exactly 1 distinct members, each in some row, none of them in column 0.
All inputs are finite; a program needn't handle non-finite values.
Results may differ from the reference program's by a relative error of at most 0.015.
Values may be sent and summed in bfloat16 or wider, within the bound.
A program may use at most 192 MiB of HBM per device.

```python
import math
import jax
import jax.numpy as jnp
from jax import lax

D = 1792
FF = 7168
TOK = 512
RATES = 8
MEMBERS = 16
LOSERS = 4
TOPS = 1
N_TP = 2


def draw_assignment(key, part):
    chosen_count = TOPS + LOSERS
    middle = jax.random.permutation(jax.random.fold_in(key, 11), MEMBERS - 2).astype(jnp.int32) + 1
    ends = jnp.array([0, MEMBERS - 1], dtype=jnp.int32)
    picked = jnp.concatenate([ends, middle[:chosen_count - 2]]).astype(jnp.int32)
    shuffle = jax.random.permutation(jax.random.fold_in(key, 13), chosen_count).astype(jnp.int32)
    order = picked[shuffle]
    winners_set = order[:TOPS]
    losers = order[TOPS:TOPS + LOSERS]
    picks = jax.random.randint(jax.random.fold_in(key, 12), (LOSERS,), 0, TOPS)
    rows = jnp.arange(LOSERS, dtype=jnp.int32)
    picks = jnp.where(rows < TOPS, rows, picks).astype(jnp.int32)
    winners = winners_set[picks]
    return jnp.stack([losers, winners], axis=1).astype(jnp.int32)


def plant(values, rng, low, largest):
    extent = values.shape
    place = [jax.random.randint(jax.random.fold_in(rng, axis), (), 0, extent[axis]) for axis in range(len(extent))]
    values = values.at[tuple(place)].set(low)
    longest = extent.index(max(extent))
    place[longest] = (place[longest] + 1) % extent[longest]
    return values.at[tuple(place)].set(largest)


def block_levels(rng, shape, pieces, least, high):
    loudness, own = 1.0, jax.random.fold_in(rng, 6)
    for axis_at, blocks in pieces:
        steps = jnp.exp(jax.random.uniform(jax.random.fold_in(own, axis_at), (blocks,), jnp.float32, least / len(pieces), high / len(pieces)))
        loudness = loudness * jnp.repeat(steps, shape[axis_at] // blocks).reshape([-1 if axis == axis_at else 1 for axis in range(len(shape))])
    return loudness


def centred(rng, dims, width, limit, shards=(), kind=jnp.bfloat16):
    drawn = width * jax.random.normal(rng, dims, jnp.float32)
    if shards:
        drawn = drawn * block_levels(rng, dims, shards, -0.22, 0.18)
    return jnp.clip(drawn, -limit, limit).astype(kind)


def setup_inputs(seed: int = 0) -> dict:
    arg_keys = jax.random.split(jax.random.key(seed), 8)
    return {
        "tokens": centred(arg_keys[0], (MEMBERS, TOK, D), 1.0, 6.0, ((0, 16), (2, 2))),
        "weight": centred(arg_keys[1], (MEMBERS, D, FF), D ** -0.5, 0.125, ((0, 16), (1, 2))),
        "momentum": centred(arg_keys[2], (MEMBERS, D, FF), 1.0, 6.0, ((0, 16), (1, 2))),
        "cotangent": centred(arg_keys[3], (MEMBERS, TOK, FF), 0.0625, 0.5, ((0, 16), (2, 2))),
        "assignment": draw_assignment(jax.random.fold_in(arg_keys[7], 71), 0),
        "lr_index": plant(jax.random.randint(arg_keys[5], (MEMBERS,), 0, RATES), jax.random.fold_in(arg_keys[5], 1), 0, RATES - 1).astype(jnp.int32),
        "rates": jnp.clip(jnp.exp(jax.random.uniform(arg_keys[6], (RATES,), jnp.float32, math.log(0.01), math.log(0.1))), 0.01, 0.1),
    }


def gelu_tanh(value):
    return jax.nn.gelu(value, approximate=True)

def reference(tokens, weight, momentum, cotangent, assignment, lr_index, rates):
    member_ids = jnp.arange(MEMBERS, dtype=jnp.int32)
    hit = assignment[:, 0][None, :] == member_ids[:, None]
    source_all = jnp.where(jnp.any(hit, axis=1), lax.optimization_barrier(jnp.sum(jnp.where(hit, assignment[:, 1][None, :], 0), axis=1)).astype(jnp.int32), member_ids)
    rate_ids = jnp.arange(RATES, dtype=jnp.int32)
    rate_all = lax.optimization_barrier(jnp.sum(jnp.where(rate_ids[None, :] == lr_index[:, None], rates[None, :], 0.0), axis=1))
    block = D // N_TP

    def one_member(member):
        source = source_all[member]
        inputs = tokens[member]
        taken_weight = weight[source]
        taken_momentum = momentum[source]
        hidden = jnp.zeros((TOK, FF), jnp.float32)
        for piece in range(N_TP):
            partial_value = jnp.dot(inputs[:, piece * block:(piece + 1) * block], taken_weight[piece * block:(piece + 1) * block], preferred_element_type=jnp.float32).astype(jnp.bfloat16)
            hidden = hidden + lax.optimization_barrier(partial_value).astype(jnp.float32)
        active, pullback = jax.vjp(gelu_tanh, hidden)
        grad_hidden = pullback(cotangent[member].astype(jnp.float32))[0].astype(jnp.bfloat16)
        grad_weight = jnp.dot(inputs.T, grad_hidden, preferred_element_type=jnp.float32)
        new_momentum = 0.9 * taken_momentum.astype(jnp.float32) + grad_weight
        updated = (taken_weight.astype(jnp.float32) - rate_all[member] * new_momentum).astype(jnp.bfloat16)
        return (active.astype(jnp.bfloat16), updated)
    activation, new_weight = lax.map(one_member, member_ids)
    return (activation, new_weight)
```

```python
import functools

import jax
import jax.numpy as jnp
from jax import lax
from jax.experimental import pallas as pl
from jax.experimental.pallas import tpu as pltpu
from jax.sharding import PartitionSpec as P

MESH = pl.DeviceIdType.MESH
ROWS = 16
PIECES = 2


def ring_of(member, members):
    core = member % 2
    y = (member // 2) % 2
    z = member // 4
    half = members // 4
    chip = z * (1 - y) + (2 * half - 1 - z) * y
    return 2 * chip + core


def member_at(place, members):
    core = place % 2
    chip = place // 2
    half = members // 4
    y = chip // half
    z = chip * (1 - y) + (2 * half - 1 - chip) * y
    return (2 * z + y) * 2 + core


def gelu_tanh(value):
    return jax.nn.gelu(value, approximate=True)


def activate(hidden, cot_block):
    active, pullback = jax.vjp(gelu_tanh, hidden)
    grad_hidden = pullback(cot_block.astype(jnp.float32))[0].astype(jnp.bfloat16)
    return (active.astype(jnp.bfloat16), grad_hidden)


def spread_kernel(members, table, own, out, came, sent, send_sem, recv_sem):
    rows, cols = own.shape
    blocks = rows // 2 // ROWS
    steps = blocks + members - 2
    width = cols // PIECES
    place = ring_of(lax.axis_index("pop"), members)
    ahead = member_at((place + 1) % members, members)
    behind = member_at((place + members - 1) % members, members)
    is_root = table[0] > 0
    chosen = table[1] > 0
    targets = (ahead, behind)

    barrier = pltpu.get_barrier_semaphore()
    for near in targets:
        pl.semaphore_signal(barrier, inc=1, device_id={"pop": near}, device_id_type=MESH)
    pl.semaphore_wait(barrier, 2)

    def copy_of(way, step, piece):
        slot = step % 2
        cut = pl.ds(piece * width, width)
        return pltpu.make_async_remote_copy(
            src_ref=sent.at[way, slot, :, cut],
            dst_ref=came.at[way, step, :, cut],
            send_sem=send_sem.at[way, slot, piece],
            recv_sem=recv_sem.at[way, step, piece],
            device_id={"pop": targets[way]},
            device_id_type=MESH,
        )

    def own_rows(way, step):
        first = way * (rows // 2) + jnp.minimum(step, blocks - 1) * ROWS
        return pl.ds(pl.multiple_of(first, ROWS), ROWS)

    for piece in range(PIECES):
        cut = pl.ds(piece * width, width)
        for way in range(2):
            sent[way, 0, :, cut] = own[way * (rows // 2) : way * (rows // 2) + ROWS, cut]
            copy_of(way, 0, piece).start()

    def forward(step, carry):
        for piece in range(PIECES):
            cut = pl.ds(piece * width, width)
            for way in range(2):
                copy_of(way, step - 1, piece).wait_recv()

                @pl.when(step >= 2)
                def _():
                    copy_of(way, step - 2, piece).wait_send()

                sent[way, step % 2, :, cut] = jnp.where(
                    is_root, own[own_rows(way, step), cut], came[way, step - 1, :, cut]
                )
                copy_of(way, step, piece).start()
        return carry

    lax.fori_loop(1, steps, forward, 0)
    for piece in range(PIECES):
        for way in range(2):
            copy_of(way, steps - 1, piece).wait_recv()
            copy_of(way, steps - 2, piece).wait_send()
            copy_of(way, steps - 1, piece).wait_send()

    def settle(block, carry):
        for way in range(2):
            at = pl.ds(pl.multiple_of(way * (rows // 2) + block * ROWS, ROWS), ROWS)
            out[at, :] = jnp.where(chosen, came[way, block + table[2 + way]], own[at, :])
        return carry

    lax.fori_loop(0, blocks, settle, 0)


def spread(value, table, members, turn):
    rows, cols = value.shape
    steps = rows // 2 // ROWS + members - 2
    return pl.pallas_call(
        functools.partial(spread_kernel, members),
        out_shape=jax.ShapeDtypeStruct(value.shape, value.dtype),
        in_specs=[
            pl.BlockSpec(memory_space=pltpu.SMEM),
            pl.BlockSpec(memory_space=pltpu.VMEM),
        ],
        out_specs=pl.BlockSpec(memory_space=pltpu.VMEM),
        scratch_shapes=[
            pltpu.VMEM((2, steps, ROWS, cols), value.dtype),
            pltpu.VMEM((2, 2, ROWS, cols), value.dtype),
            pltpu.SemaphoreType.DMA((2, 2, PIECES)),
            pltpu.SemaphoreType.DMA((2, steps, PIECES)),
        ],
        compiler_params=pltpu.CompilerParams(
            collective_id=turn, has_side_effects=True, vmem_limit_bytes=60 * 2**20
        ),
        cost_estimate=pl.CostEstimate(
            flops=0, bytes_accessed=300 * 2**20, transcendentals=0
        ),
        name=f"spread_{turn}",
    )(table, value)


def local(tokens, weight, momentum, cotangent, assignment, lr_index, rates):
    members = lax.axis_size("pop")
    ranks = lax.axis_size("tp")
    me = lax.axis_index("pop")
    side = lax.axis_index("tp")
    member_ids = jnp.arange(members, dtype=jnp.int32)
    hit = assignment[:, 0] == me
    my_source = jnp.where(jnp.any(hit), jnp.sum(jnp.where(hit, assignment[:, 1], 0)), me)
    my_index = jnp.sum(jnp.where(member_ids == me, lr_index, 0))
    rate_ids = jnp.arange(rates.shape[0], dtype=jnp.int32)
    my_rate = jnp.sum(jnp.where(rate_ids == my_index, rates, 0.0))
    tops = assignment.shape[0] // 4
    winner_hit = assignment[:, 1][None, :] == member_ids[:, None]
    present = jnp.any(winner_hit, axis=1)
    roots = jnp.sort(jnp.where(present, member_ids, members))[:tops]
    place = ring_of(me, members)
    tables = []
    for turn in range(tops):
        root = roots[turn]
        behind = (place - ring_of(root, members) + members) % members
        before = (members - behind) % members
        tables.append(
            jnp.stack(
                [
                    (me == root).astype(jnp.int32),
                    jnp.logical_and(my_source == root, me != root).astype(jnp.int32),
                    jnp.maximum(behind - 1, 0).astype(jnp.int32),
                    jnp.maximum(before - 1, 0).astype(jnp.int32),
                ]
            )
        )

    def take(value, first):
        taken = value
        for turn in range(tops):
            arrived = spread(value if turn == 0 else value + 0, tables[turn], members, first + turn)
            taken = arrived if turn == 0 else jnp.where(my_source == roots[turn], arrived, taken)
        return taken

    inputs = tokens[0]
    share_cols = cotangent.shape[2]
    taken_weight = take(weight[0], 0)
    partial_value = jnp.dot(inputs, taken_weight, preferred_element_type=jnp.float32)
    partial_value = partial_value.astype(jnp.bfloat16)
    if ranks == 2:
        swap = [(0, 1), (1, 0)]
        left, right = partial_value[:, :share_cols], partial_value[:, share_cols:]
        mine = jnp.where(side == 0, left, right)
        theirs = jnp.where(side == 0, right, left)
        theirs, raw_momentum = lax.optimization_barrier((theirs, momentum[0]))
        arrived = lax.ppermute(theirs, "tp", swap)
        taken_momentum = take(raw_momentum, tops)
        hidden = mine.astype(jnp.float32) + arrived.astype(jnp.float32)
        active, grad_mine = activate(hidden, cotangent[0])
        grad_theirs = lax.ppermute(grad_mine, "tp", swap)
        grad_hidden = jnp.concatenate(
            [
                jnp.where(side == 0, grad_mine, grad_theirs),
                jnp.where(side == 0, grad_theirs, grad_mine),
            ],
            axis=1,
        )
    else:
        taken_momentum = take(momentum[0], tops)
        hidden = lax.psum_scatter(
            partial_value, "tp", scatter_dimension=1, tiled=True
        ).astype(jnp.float32)
        active, grad_mine = activate(hidden, cotangent[0])
        grad_hidden = lax.all_gather(grad_mine, "tp", axis=1, tiled=True)
    grad_weight = lax.dot_general(
        inputs, grad_hidden, (((0,), (0,)), ((), ())), preferred_element_type=jnp.float32
    )
    new_momentum = 0.9 * taken_momentum.astype(jnp.float32) + grad_weight
    updated = (taken_weight.astype(jnp.float32) - my_rate * new_momentum).astype(jnp.bfloat16)
    return (active[None], updated[None])


def solution(mesh):
    placed = (
        P("pop", None, "tp"),
        P("pop", "tp", None),
        P("pop", "tp", None),
        P("pop", None, "tp"),
        P(),
        P(),
        P(),
    )
    return jax.shard_map(
        local,
        mesh=mesh,
        in_specs=placed,
        out_specs=(P("pop", None, "tp"), P("pop", "tp", None)),
        check_vma=False,
    )
```

```python
import functools

import jax
import jax.numpy as jnp
from jax import lax
from jax.experimental import pallas as pl
from jax.experimental.pallas import tpu as pltpu
from jax.sharding import PartitionSpec as P

MESH = pl.DeviceIdType.MESH
PIECES = 4
TILE = 512


def ring_of(member, members):
    core = member % 2
    y = (member // 2) % 2
    z = member // 4
    half = members // 4
    chip = z * (1 - y) + (2 * half - 1 - z) * y
    return 2 * chip + core


def member_at(place, members):
    core = place % 2
    chip = place // 2
    half = members // 4
    y = chip // half
    z = chip * (1 - y) + (2 * half - 1 - chip) * y
    return (2 * z + y) * 2 + core


def gelu_tanh(value):
    return jax.nn.gelu(value, approximate=True)


def activate(hidden, cot_block):
    active, pullback = jax.vjp(gelu_tanh, hidden)
    grad_hidden = pullback(cot_block.astype(jnp.float32))[0].astype(jnp.bfloat16)
    return (active.astype(jnp.bfloat16), grad_hidden)


def rows_of(rows, cols, whole_cols):
    wanted = 16 * (whole_cols // cols)
    return wanted if (rows // 2) % wanted == 0 else 16


def spread_kernel(members, ROWS, table, own, out, came, sent, send_sem, recv_sem):
    rows, cols = own.shape
    blocks = rows // 2 // ROWS
    steps = blocks + members - 2
    width = cols // PIECES
    place = ring_of(lax.axis_index("pop"), members)
    ahead = member_at((place + 1) % members, members)
    behind = member_at((place + members - 1) % members, members)
    is_root = table[0] > 0
    chosen = table[1] > 0
    targets = (ahead, behind)

    barrier = pltpu.get_barrier_semaphore()
    for near in targets:
        pl.semaphore_signal(barrier, inc=1, device_id={"pop": near}, device_id_type=MESH)
    pl.semaphore_wait(barrier, 2)

    def copy_of(way, step, piece):
        slot = step % 2
        cut = pl.ds(piece * width, width)
        return pltpu.make_async_remote_copy(
            src_ref=sent.at[way, slot, :, cut],
            dst_ref=came.at[way, step, :, cut],
            send_sem=send_sem.at[way, slot, piece],
            recv_sem=recv_sem.at[way, step, piece],
            device_id={"pop": targets[way]},
            device_id_type=MESH,
        )

    def own_rows(way, step):
        first = way * (rows // 2) + jnp.minimum(step, blocks - 1) * ROWS
        return pl.ds(pl.multiple_of(first, ROWS), ROWS)

    for piece in range(PIECES):
        cut = pl.ds(piece * width, width)
        for way in range(2):
            sent[way, 0, :, cut] = own[way * (rows // 2) : way * (rows // 2) + ROWS, cut]
            copy_of(way, 0, piece).start()

    def forward(step, carry):
        for piece in range(PIECES):
            cut = pl.ds(piece * width, width)
            for way in range(2):
                copy_of(way, step - 1, piece).wait_recv()

                @pl.when(step >= 2)
                def _():
                    copy_of(way, step - 2, piece).wait_send()

                sent[way, step % 2, :, cut] = jnp.where(
                    is_root, own[own_rows(way, step), cut], came[way, step - 1, :, cut]
                )
                copy_of(way, step, piece).start()
        return carry

    lax.fori_loop(1, steps, forward, 0)
    for piece in range(PIECES):
        for way in range(2):
            copy_of(way, steps - 1, piece).wait_recv()
            copy_of(way, steps - 2, piece).wait_send()
            copy_of(way, steps - 1, piece).wait_send()

    def settle(block, carry):
        for way in range(2):
            at = pl.ds(pl.multiple_of(way * (rows // 2) + block * ROWS, ROWS), ROWS)
            out[at, :] = jnp.where(chosen, came[way, block + table[2 + way]], own[at, :])
        return carry

    lax.fori_loop(0, blocks, settle, 0)


def spread(value, table, members, turn, part, parts):
    rows, whole_cols = value.shape
    cols = whole_cols // parts
    height = rows_of(rows, cols, whole_cols)
    steps = rows // 2 // height + members - 2
    return pl.pallas_call(
        functools.partial(spread_kernel, members, height),
        grid=(1,),
        out_shape=jax.ShapeDtypeStruct((rows, cols), value.dtype),
        in_specs=[
            pl.BlockSpec(memory_space=pltpu.SMEM),
            pl.BlockSpec((rows, cols), lambda i: (0, part), pipeline_mode=pl.Buffered(1)),
        ],
        out_specs=pl.BlockSpec((rows, cols), lambda i: (0, 0), pipeline_mode=pl.Buffered(1)),
        scratch_shapes=[
            pltpu.VMEM((2, steps, height, cols), value.dtype),
            pltpu.VMEM((2, 2, height, cols), value.dtype),
            pltpu.SemaphoreType.DMA((2, 2, PIECES)),
            pltpu.SemaphoreType.DMA((2, steps, PIECES)),
        ],
        compiler_params=pltpu.CompilerParams(
            collective_id=turn, has_side_effects=True, vmem_limit_bytes=60 * 2**20
        ),
        cost_estimate=pl.CostEstimate(
            flops=0, bytes_accessed=300 * 2**20 // parts, transcendentals=0
        ),
        name=f"spread_{turn}",
    )(table, value)


def update_kernel(half, side, rate, turned, mine, theirs, weight, first, second, out):
    block = pl.program_id(0)
    grad = jnp.where(block // half == side[0], mine[...], theirs[...])
    grad_weight = jnp.dot(turned[...], grad, preferred_element_type=jnp.float32)
    momentum = jnp.where(block < half, first[...], second[...]).astype(jnp.float32)
    new_momentum = 0.9 * momentum + grad_weight
    out[...] = (weight[...].astype(jnp.float32) - rate[0] * new_momentum).astype(out.dtype)


def update(side, rate, turned, mine, theirs, weight, first, second):
    rows, cols = weight.shape
    tokens = turned.shape[1]
    half = cols // 2 // TILE
    near = lambda j, side: (0, jnp.clip(j - side[0] * half, 0, half - 1))
    far = lambda j, side: (0, jnp.clip(j - (1 - side[0]) * half, 0, half - 1))
    return pl.pallas_call(
        functools.partial(update_kernel, half),
        grid_spec=pltpu.PrefetchScalarGridSpec(
            num_scalar_prefetch=1,
            grid=(2 * half,),
            in_specs=[
                pl.BlockSpec(memory_space=pltpu.SMEM),
                pl.BlockSpec((rows, tokens), lambda j, side: (0, 0)),
                pl.BlockSpec((tokens, TILE), near),
                pl.BlockSpec((tokens, TILE), far),
                pl.BlockSpec((rows, TILE), lambda j, side: (0, j)),
                pl.BlockSpec((rows, TILE), lambda j, side: (0, jnp.minimum(j, half - 1))),
                pl.BlockSpec((rows, TILE), lambda j, side: (0, jnp.maximum(j - half, 0))),
            ],
            out_specs=pl.BlockSpec((rows, TILE), lambda j, side: (0, j)),
        ),
        out_shape=jax.ShapeDtypeStruct(weight.shape, weight.dtype),
        compiler_params=pltpu.CompilerParams(vmem_limit_bytes=40 * 2**20),
        cost_estimate=pl.CostEstimate(
            flops=2 * rows * cols * tokens,
            bytes_accessed=6 * rows * cols,
            transcendentals=0,
        ),
        name="update",
    )(side, rate, turned, mine, theirs, weight, first, second)


def local(tokens, weight, momentum, cotangent, assignment, lr_index, rates):
    members = lax.axis_size("pop")
    ranks = lax.axis_size("tp")
    me = lax.axis_index("pop")
    side = lax.axis_index("tp")
    member_ids = jnp.arange(members, dtype=jnp.int32)
    hit = assignment[:, 0] == me
    my_source = jnp.where(jnp.any(hit), jnp.sum(jnp.where(hit, assignment[:, 1], 0)), me)
    my_index = jnp.sum(jnp.where(member_ids == me, lr_index, 0))
    rate_ids = jnp.arange(rates.shape[0], dtype=jnp.int32)
    my_rate = jnp.sum(jnp.where(rate_ids == my_index, rates, 0.0))
    tops = assignment.shape[0] // 4
    winner_hit = assignment[:, 1][None, :] == member_ids[:, None]
    present = jnp.any(winner_hit, axis=1)
    roots = jnp.sort(jnp.where(present, member_ids, members))[:tops]
    place = ring_of(me, members)
    tables = []
    for turn in range(tops):
        root = roots[turn]
        behind = (place - ring_of(root, members) + members) % members
        before = (members - behind) % members
        tables.append(
            jnp.stack(
                [
                    (me == root).astype(jnp.int32),
                    jnp.logical_and(my_source == root, me != root).astype(jnp.int32),
                    jnp.maximum(behind - 1, 0).astype(jnp.int32),
                    jnp.maximum(before - 1, 0).astype(jnp.int32),
                ]
            )
        )

    def take(value, first, part=0, parts=1):
        taken = None
        for turn in range(tops):
            arrived = spread(value, tables[turn], members, first + turn, part, parts)
            if taken is None:
                taken = arrived
            else:
                taken = jnp.where(my_source == roots[turn], arrived, taken)
        return taken

    inputs = tokens[0]
    share_cols = cotangent.shape[2]
    taken_weight = take(weight[0], 0)
    partial_value = jnp.dot(inputs, taken_weight, preferred_element_type=jnp.float32)
    partial_value = partial_value.astype(jnp.bfloat16)
    if ranks == 2:
        swap = [(0, 1), (1, 0)]
        left, right = partial_value[:, :share_cols], partial_value[:, share_cols:]
        mine = jnp.where(side == 0, left, right)
        theirs = jnp.where(side == 0, right, left)
        theirs, raw_momentum = lax.optimization_barrier((theirs, momentum[0]))
        arrived = lax.ppermute(theirs, "tp", swap)
        first = take(raw_momentum, tops, 0, 2)
        arrived, first = lax.optimization_barrier((arrived, first))
        hidden = mine.astype(jnp.float32) + arrived.astype(jnp.float32)
        active, grad_mine = activate(hidden, cotangent[0])
        grad_mine, raw_momentum = lax.optimization_barrier((grad_mine, raw_momentum))
        grad_theirs = lax.ppermute(grad_mine, "tp", swap)
        second = take(raw_momentum, 2 * tops, 1, 2)
        updated = update(
            side.astype(jnp.int32).reshape(1),
            my_rate.reshape(1),
            inputs.T,
            grad_mine,
            grad_theirs,
            taken_weight,
            first,
            second,
        )
    else:
        taken_momentum = take(momentum[0], tops)
        hidden = lax.psum_scatter(
            partial_value, "tp", scatter_dimension=1, tiled=True
        ).astype(jnp.float32)
        active, grad_mine = activate(hidden, cotangent[0])
        grad_hidden = lax.all_gather(grad_mine, "tp", axis=1, tiled=True)
        grad_weight = lax.dot_general(
            inputs, grad_hidden, (((0,), (0,)), ((), ())), preferred_element_type=jnp.float32
        )
        new_momentum = 0.9 * taken_momentum.astype(jnp.float32) + grad_weight
        updated = taken_weight.astype(jnp.float32) - my_rate * new_momentum
        updated = updated.astype(jnp.bfloat16)
    return (active[None], updated[None])


def solution(mesh):
    placed = (
        P("pop", None, "tp"),
        P("pop", "tp", None),
        P("pop", "tp", None),
        P("pop", None, "tp"),
        P(),
        P(),
        P(),
    )
    return jax.shard_map(
        local,
        mesh=mesh,
        in_specs=placed,
        out_specs=(P("pop", None, "tp"), P("pop", "tp", None)),
        check_vma=False,
    )
```

```python
import functools

import jax
import jax.numpy as jnp
from jax import lax
from jax.experimental import pallas as pl
from jax.experimental.pallas import tpu as pltpu
from jax.sharding import PartitionSpec as P

MESH = pl.DeviceIdType.MESH
PIECES = 4
TILE = 512


def ring_of(member, members):
    core = member % 2
    y = (member // 2) % 2
    z = member // 4
    half = members // 4
    chip = z * (1 - y) + (2 * half - 1 - z) * y
    return 2 * chip + core


def member_at(place, members):
    core = place % 2
    chip = place // 2
    half = members // 4
    y = chip // half
    z = chip * (1 - y) + (2 * half - 1 - chip) * y
    return (2 * z + y) * 2 + core


def gelu_tanh(value):
    return jax.nn.gelu(value, approximate=True)


def activate(hidden, cot_block):
    active, pullback = jax.vjp(gelu_tanh, hidden)
    grad_hidden = pullback(cot_block.astype(jnp.float32))[0].astype(jnp.bfloat16)
    return (active.astype(jnp.bfloat16), grad_hidden)


def rows_of(rows, cols, whole_cols):
    wanted = 16 * (whole_cols // cols)
    return wanted if (rows // 2) % wanted == 0 else 16


def spread_kernel(
    members, height, table, own, out, came, mirror, other, sent,
    send_sem, recv_sem, near_send, near_recv, back_send, back_recv,
):
    rows, cols = own.shape
    half = rows // 2
    blocks = half // height
    chips = members // 2
    steps = blocks + chips - 1
    width = cols // PIECES
    place = ring_of(lax.axis_index("pop"), members)
    chip = place // 2
    core = place % 2
    target = member_at(2 * ((chip + 1 - 2 * core + chips) % chips) + core, members)
    origin = member_at(2 * ((chip - 1 + 2 * core + chips) % chips) + core, members)
    partner = member_at(2 * chip + 1 - core, members)
    is_root = table[0] > 0
    chosen = table[1] > 0
    partner_root = table[4] > 0

    barrier = pltpu.get_barrier_semaphore()
    for near in (target, origin, partner):
        pl.semaphore_signal(barrier, inc=1, device_id={"pop": near}, device_id_type=MESH)
    pl.semaphore_wait(barrier, 3)

    def block_rows(way, block):
        return pl.ds(pl.multiple_of(way * half + block * height, height), height)

    def lend(block):
        return pltpu.make_async_remote_copy(
            src_ref=own.at[block_rows(1 - core, block), :],
            dst_ref=other.at[block],
            send_sem=near_send.at[block],
            recv_sem=near_recv.at[block],
            device_id={"pop": partner},
            device_id_type=MESH,
        )

    def onward(step, piece):
        cut = pl.ds(piece * width, width)
        return pltpu.make_async_remote_copy(
            src_ref=sent.at[step % 2, :, cut],
            dst_ref=came.at[step, :, cut],
            send_sem=send_sem.at[step % 2, piece],
            recv_sem=recv_sem.at[step, piece],
            device_id={"pop": target},
            device_id_type=MESH,
        )

    def across(step):
        return pltpu.make_async_remote_copy(
            src_ref=came.at[step],
            dst_ref=mirror.at[step],
            send_sem=back_send.at[step],
            recv_sem=back_recv.at[step],
            device_id={"pop": partner},
            device_id_type=MESH,
        )

    def each(count, act):
        def body(index, carry):
            act(index)
            return carry

        lax.fori_loop(0, count, body, 0)

    each(blocks, lambda block: lend(block).start())
    lend(0).wait_recv()
    for piece in range(PIECES):
        cut = pl.ds(piece * width, width)
        sent[0, :, cut] = jnp.where(is_root, own[block_rows(core, 0), cut], other[0, :, cut])
        onward(0, piece).start()

    def forward(step, carry):
        block = jnp.minimum(step, blocks - 1)

        @pl.when(step < blocks)
        def _():
            lend(step).wait_recv()

        for piece in range(PIECES):
            cut = pl.ds(piece * width, width)
            onward(step - 1, piece).wait_recv()

            @pl.when(step >= 2)
            def _():
                onward(step - 2, piece).wait_send()

            relayed = jnp.where(partner_root, other[block, :, cut], came[step - 1, :, cut])
            sent[step % 2, :, cut] = jnp.where(
                is_root, own[block_rows(core, block), cut], relayed
            )
            onward(step, piece).start()
        across(step - 1).start()
        return carry

    lax.fori_loop(1, steps, forward, 0)
    for piece in range(PIECES):
        onward(steps - 1, piece).wait_recv()
    across(steps - 1).start()

    def settle(block):
        at = block_rows(core, block)
        out[at, :] = jnp.where(chosen, came[block + table[2 + core]], own[at, :])

    each(blocks, settle)
    each(steps, lambda step: across(step).wait_recv())

    def settle_other(block):
        at = block_rows(1 - core, block)
        out[at, :] = jnp.where(chosen, mirror[block + table[3 - core]], own[at, :])

    each(blocks, settle_other)
    for piece in range(PIECES):
        onward(steps - 2, piece).wait_send()
        onward(steps - 1, piece).wait_send()
    each(blocks, lambda block: lend(block).wait_send())
    each(steps, lambda step: across(step).wait_send())


def spread(value, table, members, turn, part, parts):
    rows, whole_cols = value.shape
    cols = whole_cols // parts
    height = rows_of(rows, cols, whole_cols)
    blocks = rows // 2 // height
    steps = blocks + members // 2 - 1
    return pl.pallas_call(
        functools.partial(spread_kernel, members, height),
        grid=(1,),
        out_shape=jax.ShapeDtypeStruct((rows, cols), value.dtype),
        in_specs=[
            pl.BlockSpec(memory_space=pltpu.SMEM),
            pl.BlockSpec((rows, cols), lambda i: (0, part), pipeline_mode=pl.Buffered(1)),
        ],
        out_specs=pl.BlockSpec((rows, cols), lambda i: (0, 0), pipeline_mode=pl.Buffered(1)),
        scratch_shapes=[
            pltpu.VMEM((steps, height, cols), value.dtype),
            pltpu.VMEM((steps, height, cols), value.dtype),
            pltpu.VMEM((blocks, height, cols), value.dtype),
            pltpu.VMEM((2, height, cols), value.dtype),
            pltpu.SemaphoreType.DMA((2, PIECES)),
            pltpu.SemaphoreType.DMA((steps, PIECES)),
            pltpu.SemaphoreType.DMA((blocks,)),
            pltpu.SemaphoreType.DMA((blocks,)),
            pltpu.SemaphoreType.DMA((steps,)),
            pltpu.SemaphoreType.DMA((steps,)),
        ],
        compiler_params=pltpu.CompilerParams(
            collective_id=turn, has_side_effects=True, vmem_limit_bytes=60 * 2**20
        ),
        cost_estimate=pl.CostEstimate(
            flops=0, bytes_accessed=300 * 2**20 // parts, transcendentals=0
        ),
        name=f"spread_{turn}",
    )(table, value)


def update_kernel(half, side, rate, turned, mine, theirs, weight, first, second, out):
    block = pl.program_id(0)
    grad = jnp.where(block // half == side[0], mine[...], theirs[...])
    grad_weight = jnp.dot(turned[...], grad, preferred_element_type=jnp.float32)
    momentum = jnp.where(block < half, first[...], second[...]).astype(jnp.float32)
    new_momentum = 0.9 * momentum + grad_weight
    out[...] = (weight[...].astype(jnp.float32) - rate[0] * new_momentum).astype(out.dtype)


def update(side, rate, turned, mine, theirs, weight, first, second):
    rows, cols = weight.shape
    tokens = turned.shape[1]
    half = cols // 2 // TILE
    near = lambda j, side: (0, jnp.clip(j - side[0] * half, 0, half - 1))
    far = lambda j, side: (0, jnp.clip(j - (1 - side[0]) * half, 0, half - 1))
    return pl.pallas_call(
        functools.partial(update_kernel, half),
        grid_spec=pltpu.PrefetchScalarGridSpec(
            num_scalar_prefetch=1,
            grid=(2 * half,),
            in_specs=[
                pl.BlockSpec(memory_space=pltpu.SMEM),
                pl.BlockSpec((rows, tokens), lambda j, side: (0, 0)),
                pl.BlockSpec((tokens, TILE), near),
                pl.BlockSpec((tokens, TILE), far),
                pl.BlockSpec((rows, TILE), lambda j, side: (0, j)),
                pl.BlockSpec((rows, TILE), lambda j, side: (0, jnp.minimum(j, half - 1))),
                pl.BlockSpec((rows, TILE), lambda j, side: (0, jnp.maximum(j - half, 0))),
            ],
            out_specs=pl.BlockSpec((rows, TILE), lambda j, side: (0, j)),
        ),
        out_shape=jax.ShapeDtypeStruct(weight.shape, weight.dtype),
        compiler_params=pltpu.CompilerParams(vmem_limit_bytes=40 * 2**20),
        cost_estimate=pl.CostEstimate(
            flops=2 * rows * cols * tokens,
            bytes_accessed=6 * rows * cols,
            transcendentals=0,
        ),
        name="update",
    )(side, rate, turned, mine, theirs, weight, first, second)


def local(tokens, weight, momentum, cotangent, assignment, lr_index, rates):
    members = lax.axis_size("pop")
    ranks = lax.axis_size("tp")
    me = lax.axis_index("pop")
    side = lax.axis_index("tp")
    member_ids = jnp.arange(members, dtype=jnp.int32)
    hit = assignment[:, 0] == me
    my_source = jnp.where(jnp.any(hit), jnp.sum(jnp.where(hit, assignment[:, 1], 0)), me)
    my_index = jnp.sum(jnp.where(member_ids == me, lr_index, 0))
    rate_ids = jnp.arange(rates.shape[0], dtype=jnp.int32)
    my_rate = jnp.sum(jnp.where(rate_ids == my_index, rates, 0.0))
    tops = assignment.shape[0] // 4
    winner_hit = assignment[:, 1][None, :] == member_ids[:, None]
    present = jnp.any(winner_hit, axis=1)
    roots = jnp.sort(jnp.where(present, member_ids, members))[:tops]
    place = ring_of(me, members)
    tables = []
    for turn in range(tops):
        root = roots[turn]
        chips = members // 2
        root_place = ring_of(root, members)
        behind = (place // 2 - root_place // 2 + chips) % chips
        entries = (
            me == root,
            jnp.logical_and(my_source == root, me != root),
            (behind + chips - 1) % chips,
            (2 * chips - behind - 1) % chips,
            jnp.logical_and(place // 2 == root_place // 2, me != root),
        )
        tables.append(jnp.stack([entry.astype(jnp.int32) for entry in entries]))

    def take(value, first, part=0, parts=1):
        taken = None
        for turn in range(tops):
            arrived = spread(value, tables[turn], members, first + turn, part, parts)
            if taken is None:
                taken = arrived
            else:
                taken = jnp.where(my_source == roots[turn], arrived, taken)
        return taken

    inputs = tokens[0]
    share_cols = cotangent.shape[2]
    taken_weight = take(weight[0], 0)
    partial_value = jnp.dot(inputs, taken_weight, preferred_element_type=jnp.float32)
    partial_value = partial_value.astype(jnp.bfloat16)
    if ranks == 2:
        swap = [(0, 1), (1, 0)]
        left, right = partial_value[:, :share_cols], partial_value[:, share_cols:]
        mine = jnp.where(side == 0, left, right)
        theirs = jnp.where(side == 0, right, left)
        theirs, raw_momentum = lax.optimization_barrier((theirs, momentum[0]))
        arrived = lax.ppermute(theirs, "tp", swap)
        first = take(raw_momentum, tops, 0, 2)
        arrived, first = lax.optimization_barrier((arrived, first))
        hidden = mine.astype(jnp.float32) + arrived.astype(jnp.float32)
        active, grad_mine = activate(hidden, cotangent[0])
        grad_mine, raw_momentum = lax.optimization_barrier((grad_mine, raw_momentum))
        grad_theirs = lax.ppermute(grad_mine, "tp", swap)
        second = take(raw_momentum, 2 * tops, 1, 2)
        updated = update(
            side.astype(jnp.int32).reshape(1),
            my_rate.reshape(1),
            inputs.T,
            grad_mine,
            grad_theirs,
            taken_weight,
            first,
            second,
        )
    else:
        taken_momentum = take(momentum[0], tops)
        hidden = lax.psum_scatter(
            partial_value, "tp", scatter_dimension=1, tiled=True
        ).astype(jnp.float32)
        active, grad_mine = activate(hidden, cotangent[0])
        grad_hidden = lax.all_gather(grad_mine, "tp", axis=1, tiled=True)
        grad_weight = lax.dot_general(
            inputs, grad_hidden, (((0,), (0,)), ((), ())), preferred_element_type=jnp.float32
        )
        new_momentum = 0.9 * taken_momentum.astype(jnp.float32) + grad_weight
        updated = taken_weight.astype(jnp.float32) - my_rate * new_momentum
        updated = updated.astype(jnp.bfloat16)
    return (active[None], updated[None])


def solution(mesh):
    placed = (
        P("pop", None, "tp"),
        P("pop", "tp", None),
        P("pop", "tp", None),
        P("pop", None, "tp"),
        P(),
        P(),
        P(),
    )
    return jax.shard_map(
        local,
        mesh=mesh,
        in_specs=placed,
        out_specs=(P("pop", None, "tp"), P("pop", "tp", None)),
        check_vma=False,
    )
```
